512 devices in a mesh: row: 32 (over z_hi, y, core), col: 16 (over z_lo, x).
Axes of the slice: x: 4, y: 8, z: 8 (z_hi: 2, z_lo: 4; z = z_hi * 4 + z_lo), core: 2. Of those that a mesh axis runs over, the one named last changes fastest.
Arguments:
- features: float32 [24576, 256], P(('row', 'col')), may hold values from -6 to 6
- inv_scale: float32 [256], replicated, may hold values from 0.001953125 to 0.015625
- probe_u: float32 [24576, 64], P(('row', 'col')), may hold values from -6 to 6
- solve_v: float32 [24576, 64], P(('row', 'col')), may hold values from -6 to 6
Outputs:
- feature_grad: float32 [24576, 256], P(('row', 'col'))
The draws below stay inside these ranges and needn't reach their ends.
All inputs are finite; a program needn't handle non-finite values.
Results may differ from the reference program's by a relative error of at most 0.0003.
Values sent between devices are 32-bit elements; how exact they have to be, the bound alone decides.
No kernel may reach another device: no remote copies, remote signals or barrier semaphores. Data moves between devices by JAX's collectives and lax.ppermute only.
A program may use at most 64 MiB of HBM per device.

```python
import math
import jax
import jax.numpy as jnp
from jax import lax

P_DEV = 48
F = 256
RANK = 64
N = 24576
N_COL = 16


def block_scale(key, dims, shards, least, largest):
    level, own = 1.0, jax.random.fold_in(key, 6)
    for dim, parts in shards:
        heights = jnp.exp(jax.random.uniform(jax.random.fold_in(own, dim), (parts,), jnp.float32, least / len(shards), largest / len(shards)))
        level = level * jnp.repeat(heights, dims[dim] // parts).reshape([-1 if axis == dim else 1 for axis in range(len(dims))])
    return level


def centred(key, dims, scale, most, cuts=(), kind=jnp.bfloat16):
    array = jax.random.normal(key, dims, jnp.float32) * scale
    if len(cuts) > 0:
        array = block_scale(key, dims, cuts, -0.22, 0.18) * array
    return jnp.clip(array, min=-most, max=most).astype(kind)


def setup_inputs(seed: int = 0) -> dict:
    key_of = jax.random.split(jax.random.key(seed), 5)
    features = centred(key_of[0], (N, F), 1.0, 6.0, ((0, 512),), jnp.float32)
    inv_scale = jnp.clip(jnp.exp(jax.random.uniform(key_of[1], (F,), jnp.float32, math.log(0.001953125), math.log(0.015625))), 0.001953125, 0.015625)
    probe_u = centred(key_of[2], (N, RANK), 1.0, 6.0, ((0, 512),), jnp.float32)
    solve_v = centred(key_of[3], (N, RANK), 1.0, 6.0, ((0, 512),), jnp.float32)
    return {"features": features, "inv_scale": inv_scale, "probe_u": probe_u, "solve_v": solve_v}


def reference(features, inv_scale, probe_u, solve_v):
    block_rows = P_DEV * N_COL
    blocks_count = features.shape[0] // block_rows
    scaled = features * inv_scale
    squares = jnp.sum(scaled * features, axis=1)
    left_all = jnp.concatenate([probe_u, solve_v], axis=1)
    right_all = jnp.concatenate([solve_v, probe_u], axis=1)

    def row_block(index):
        offset = (index * block_rows).astype(jnp.int32)
        row_x = lax.dynamic_slice_in_dim(features, offset, block_rows, 0)
        row_left = lax.dynamic_slice_in_dim(left_all, offset, block_rows, 0)
        row_sq = lax.dynamic_slice_in_dim(squares, offset, block_rows, 0)
        inner_prod = jnp.dot(row_x, scaled.T, precision=lax.Precision.HIGHEST, preferred_element_type=jnp.float32)
        distance = row_sq[:, None] + squares[None, :] - 2.0 * inner_prod
        kernel = jnp.exp(-0.5 * distance)
        mixing = jnp.dot(row_left, right_all.T, precision=lax.Precision.HIGHEST, preferred_element_type=jnp.float32)
        coupling = mixing * kernel
        pulled = jnp.dot(coupling, features, precision=lax.Precision.HIGHEST, preferred_element_type=jnp.float32)
        row_sums = jnp.sum(coupling, axis=1)
        return (pulled - row_sums[:, None] * row_x) * inv_scale

    result = lax.map(row_block, jnp.arange(blocks_count, dtype=jnp.int32))
    return result.reshape(features.shape[0], features.shape[1])
```

```python
import functools

import jax
import jax.numpy as jnp
from jax import lax
from jax.experimental import pallas as pl
from jax.experimental.pallas import tpu as pltpu
from jax.sharding import Mesh, PartitionSpec as P

NT = (((1,), (1,)), ((), ()))
NN = (((1,), (0,)), ((), ()))

AXES = ("zh", "yh", "yl", "core", "zm", "zb", "x")
SIZES = (2, 4, 2, 2, 2, 2, 4)
BRICK = ("yl", "zb", "x")
FAR = ("yh", "zh", "zm")


def split(a):
    hi = a.astype(jnp.bfloat16)
    return hi, (a - hi.astype(jnp.float32)).astype(jnp.bfloat16)


def dot(a, b, dims):
    return lax.dot_general(a, b, dims, preferred_element_type=jnp.float32)


def tile_kernel(first, last, inv_ref, row_ref, col_ref, *refs):
    if first:
        out_ref, sum_ref, row_x3, row_w3, row_q, row_sum = refs
    else:
        acc_ref, acc_sum_ref, out_ref, row_x3, row_w3, row_q, row_sum = refs
    step = pl.program_id(0)
    width = inv_ref.shape[1]
    rank = (row_ref.shape[1] - width) // 2
    inv = inv_ref[...]

    @pl.when(step == 0)
    def _():
        x = row_ref[:, :width]
        scaled = x * inv
        hi, lo = split(scaled)
        row_x3[...] = jnp.concatenate([hi, lo, hi], axis=1)
        row_q[...] = jnp.broadcast_to(
            -0.5 * jnp.sum(scaled * x, axis=1, keepdims=True), row_q.shape
        )
        hi, lo = split(pltpu.roll(row_ref[:, width:], rank, 1))
        row_w3[...] = jnp.concatenate([hi, lo, hi], axis=1)
        if first:
            out_ref[...] = jnp.zeros_like(out_ref)
            row_sum[...] = jnp.zeros_like(row_sum)
        else:
            out_ref[...] = acc_ref[...]
            row_sum[...] = acc_sum_ref[...]

    col_x = col_ref[:, :width]
    x_hi, x_lo = split(col_x)
    w_hi, w_lo = split(col_ref[:, width:])
    col_q = lax.dot_general(
        jnp.full((8, width), -0.5, jnp.float32),
        col_x * col_x * inv,
        NT,
        precision=lax.Precision.HIGHEST,
        preferred_element_type=jnp.float32,
    )[:1]
    inner = dot(row_x3[...], jnp.concatenate([x_hi, x_hi, x_lo], axis=1), NT)
    mixing = dot(row_w3[...], jnp.concatenate([w_hi, w_hi, w_lo], axis=1), NT)
    lanes = row_q.shape[1]
    parts = col_x.shape[0] // lanes
    q = jnp.concatenate([row_q[...]] * parts, axis=1) + col_q
    coupling = mixing * jnp.exp(inner + q)
    c_hi, c_lo = split(coupling)
    sums = row_sum[...]
    for part in range(parts):
        sums = sums + coupling[:, part * lanes : (part + 1) * lanes]
    row_sum[...] = sums
    out_ref[...] += dot(
        jnp.concatenate([c_hi, c_lo, c_hi], axis=1),
        jnp.concatenate([x_hi, x_hi, x_lo], axis=0),
        NN,
    )

    @pl.when(step == pl.num_programs(0) - 1)
    def _():
        if last:
            total = jnp.sum(row_sum[...], axis=1, keepdims=True)
            out_ref[...] = (out_ref[...] - total * row_ref[:, :width]) * inv
        else:
            sum_ref[...] = row_sum[...]


def tile_terms(inv_scale, rows, cols, chunk, before=None):
    width = inv_scale.shape[0]
    n_rows, packed = rows.shape
    rank2 = packed - width
    first = before is None
    whole = lambda lanes: pl.BlockSpec((n_rows, lanes), lambda j: (0, 0))
    shape = lambda lanes: jax.ShapeDtypeStruct((n_rows, lanes), jnp.float32)
    specs = [
        pl.BlockSpec((1, width), lambda j: (0, 0)),
        whole(packed),
        pl.BlockSpec((chunk, packed), lambda j: (j, 0)),
    ]
    return pl.pallas_call(
        functools.partial(tile_kernel, first, not first),
        grid=(cols.shape[0] // chunk,),
        in_specs=specs if first else [*specs, whole(width), whole(128)],
        out_specs=[whole(width), whole(128)] if first else whole(width),
        out_shape=[shape(width), shape(128)] if first else shape(width),
        scratch_shapes=[
            pltpu.VMEM((n_rows, 3 * width), jnp.bfloat16),
            pltpu.VMEM((n_rows, 3 * rank2), jnp.bfloat16),
            pltpu.VMEM((n_rows, 128), jnp.float32),
            pltpu.VMEM((n_rows, 128), jnp.float32),
        ],
    )(inv_scale.reshape(1, width), rows, cols, *(before or ()))


def spread(block, axes, count):
    copies = jnp.broadcast_to(block[None], (count, *block.shape))
    return lax.all_to_all(copies, axes, 0, 0, tiled=True)


def on_device(features, inv_scale, probe_u, solve_v):
    local, width = features.shape
    own = jnp.concatenate([features, probe_u, solve_v], axis=1)
    cols = spread(own, FAR, 16).reshape(16 * local, -1)
    other = lax.ppermute(cols, "core", [(0, 1), (1, 0)])
    rows = spread(own, BRICK, 16).reshape(16 * local, -1)
    begun = tile_terms(inv_scale, rows, cols, 384)
    terms = tile_terms(inv_scale, rows, other, 384, begun)
    shares = lax.all_to_all(terms.reshape(16, local, width), BRICK, 0, 0, tiled=True)
    return jnp.sum(shares, axis=0)


def solution(mesh):
    parts = Mesh(mesh.devices.reshape(SIZES), AXES)
    return jax.shard_map(
        on_device,
        mesh=parts,
        in_specs=(P(AXES, None), P(), P(AXES, None), P(AXES, None)),
        out_specs=P(AXES, None),
        check_vma=False,
    )
```

```python
import jax
import jax.numpy as jnp
from jax import lax
from jax.experimental import pallas as pl
from jax.experimental.pallas import tpu as pltpu
from jax.sharding import Mesh, PartitionSpec as P

NT = (((1,), (1,)), ((), ()))
NN = (((1,), (0,)), ((), ()))
LANES = 128
CHUNK = 384

AXIS = "device"
COORDS = tuple(
    (x, y, 4 * z_hi + z_lo, core)
    for z_hi in range(2)
    for y in range(8)
    for core in range(2)
    for z_lo in range(4)
    for x in range(4)
)


def groups(key, place):
    found = {}
    for device, at in enumerate(COORDS):
        found.setdefault(key(*at), []).append((place(*at), device))
    return [[device for _, device in sorted(found[k])] for k in sorted(found)]


def pairs(move):
    index = {at: device for device, at in enumerate(COORDS)}
    return [(device, index[move(*at)]) for device, at in enumerate(COORDS)]


BRICK = groups(
    lambda x, y, z, c: (y // 2, z // 2, c), lambda x, y, z, c: (x, y % 2, z % 2)
)
PLACES = [
    [
        4 * ((x - shift) % 4) + (2 * (y % 2) + z % 2 ^ other)
        for shift in (0, 1, -1, 2)
        for other in range(4)
    ]
    for x, y, z, _ in COORDS
]
STRANDS = ((0, 2, 5, 7), (1, 3, 4, 6))
STRAND = tuple(int(place in STRANDS[1]) for place in range(8))
FAR_Y = lambda x, y, z, c: (c, x, STRAND[y], z)
FAR_Z = lambda x, y, z, c: (c, x, y, STRAND[z])
FAR_FIRST = groups(
    lambda *at: FAR_Z(*at) if at[3] else FAR_Y(*at), lambda x, y, z, c: z if c else y
)
FAR_SECOND = groups(
    lambda *at: FAR_Y(*at) if at[3] else FAR_Z(*at), lambda x, y, z, c: y if c else z
)


def split(a):
    hi = a.astype(jnp.bfloat16)
    return hi, (a - hi.astype(jnp.float32)).astype(jnp.bfloat16)


def dot(a, b, dims):
    return lax.dot_general(a, b, dims, preferred_element_type=jnp.float32)


def tile_kernel(place_ref, inv_ref, r0, r1, r2, r3, near_ref, other_ref, out_ref, row_x, row_x3, row_w3):
    width = inv_ref.shape[1]
    rank = (near_ref.shape[1] - width) // 2
    inv = inv_ref[...]
    for k, row_ref in enumerate((r0, r1, r2, r3)):
        count = row_ref.shape[0] // 4
        for q in range(4):
            row = row_ref[q * count : (q + 1) * count, :]
            start = pl.multiple_of(place_ref[4 * k + q] * count, count)
            where = pl.ds(start, count)
            x = row[:, :width]
            row_x[where, :] = x
            hi, lo = split(x * inv)
            row_x3[where, :] = jnp.concatenate([hi, lo, hi], axis=1)
            hi, lo = split(pltpu.roll(row[:, width:], rank, 1))
            row_w3[where, :] = jnp.concatenate([hi, lo, hi], axis=1)
    x = row_x[...]
    row_q = jnp.broadcast_to(
        -0.5 * jnp.sum(x * inv * x, axis=1, keepdims=True), (x.shape[0], LANES)
    )
    sums = None
    for col_ref in (near_ref, other_ref):
        for start in range(0, col_ref.shape[0], CHUNK):
            col = col_ref[start : start + CHUNK, :]
            col_x = col[:, :width]
            x_hi, x_lo = split(col_x)
            w_hi, w_lo = split(col[:, width:])
            col_q = lax.dot_general(
                jnp.full((8, width), -0.5, jnp.float32),
                col_x * col_x * inv,
                NT,
                precision=lax.Precision.HIGHEST,
                preferred_element_type=jnp.float32,
            )[:1]
            inner = dot(row_x3[...], jnp.concatenate([x_hi, x_hi, x_lo], axis=1), NT)
            mixing = dot(row_w3[...], jnp.concatenate([w_hi, w_hi, w_lo], axis=1), NT)
            parts = col.shape[0] // LANES
            q = jnp.concatenate([row_q] * parts, axis=1) + col_q
            coupling = mixing * jnp.exp(inner + q)
            c_hi, c_lo = split(coupling)
            for part in range(parts):
                piece = coupling[:, part * LANES : (part + 1) * LANES]
                sums = piece if sums is None else sums + piece
            pulled = dot(
                jnp.concatenate([c_hi, c_lo, c_hi], axis=1),
                jnp.concatenate([x_hi, x_hi, x_lo], axis=0),
                NN,
            )
            if col_ref is near_ref and start == 0:
                out_ref[...] = pulled
            else:
                out_ref[...] += pulled
    total = jnp.sum(sums, axis=1, keepdims=True)
    out_ref[...] = (out_ref[...] - total * row_x[...]) * inv


def tile_terms(inv_scale, places, rows, near, other):
    width = inv_scale.shape[0]
    packed = near.shape[1]
    count = sum(block.shape[0] for block in rows)
    vmem = pl.BlockSpec(memory_space=pltpu.VMEM)
    return pl.pallas_call(
        tile_kernel,
        in_specs=[pl.BlockSpec(memory_space=pltpu.SMEM)] + [vmem] * 7,
        out_specs=vmem,
        out_shape=jax.ShapeDtypeStruct((count, width), jnp.float32),
        scratch_shapes=[
            pltpu.VMEM((count, width), jnp.float32),
            pltpu.VMEM((count, 3 * width), jnp.bfloat16),
            pltpu.VMEM((count, 3 * (packed - width)), jnp.bfloat16),
        ],
    )(places, inv_scale.reshape(1, width), *rows, near, other)


def exchange(blocks, members):
    return lax.all_to_all(blocks, AXIS, 0, 0, axis_index_groups=members, tiled=True)


def spread(block, members):
    copies = jnp.broadcast_to(block[None], (len(members[0]), *block.shape))
    return exchange(copies, members).reshape(-1, block.shape[-1])


def send(block, move):
    return lax.ppermute(block, AXIS, pairs(move))


def on_device(features, inv_scale, probe_u, solve_v):
    local, width = features.shape
    own = jnp.concatenate([features, probe_u, solve_v], axis=1)
    far, *partners = lax.optimization_barrier(
        (
            spread(own, FAR_FIRST),
            send(own, lambda x, y, z, c: (x, y, z ^ 1, c)),
            send(own, lambda x, y, z, c: (x, y ^ 1, z, c)),
            send(own, lambda x, y, z, c: (x, y ^ 1, z ^ 1, c)),
        )
    )
    quad = jnp.concatenate([own, *partners])
    near, *ring = lax.optimization_barrier(
        (
            spread(far, FAR_SECOND),
            send(quad, lambda x, y, z, c: ((x + 1) % 4, y, z, c)),
            send(quad, lambda x, y, z, c: ((x - 1) % 4, y, z, c)),
            send(quad, lambda x, y, z, c: ((x + 2) % 4, y, z, c)),
        )
    )
    other = send(near, lambda x, y, z, c: (x, y, z, 1 - c))
    places = jnp.asarray(PLACES, jnp.int32)[lax.axis_index(AXIS)]
    terms = tile_terms(inv_scale, places, [quad, *ring], near, other)
    shares = exchange(terms.reshape(len(BRICK[0]), local, width), BRICK)
    return jnp.sum(shares, axis=0)


def solution(mesh):
    return jax.shard_map(
        on_device,
        mesh=Mesh(mesh.devices.reshape(-1), (AXIS,)),
        in_specs=(P(AXIS, None), P(), P(AXIS, None), P(AXIS, None)),
        out_specs=P(AXIS, None),
        check_vma=False,
    )
```

```python
import jax
import jax.numpy as jnp
from jax import lax
from jax.experimental import pallas as pl
from jax.experimental.pallas import tpu as pltpu
from jax.sharding import Mesh, PartitionSpec as P

NT = (((1,), (1,)), ((), ()))
NN = (((1,), (0,)), ((), ()))
LANES = 128
CHUNK = 256

AXIS = "device"
SHIFTS = (0, 1, -1, 2)
COORDS = tuple(
    (x, y, 4 * z_hi + z_lo, core)
    for z_hi in range(2)
    for y in range(8)
    for core in range(2)
    for z_lo in range(4)
    for x in range(4)
)


def groups(key, place):
    found = {}
    for device, at in enumerate(COORDS):
        found.setdefault(key(*at), []).append((place(*at), device))
    return [[device for _, device in sorted(found[k])] for k in sorted(found)]


def pairs(move):
    index = {at: device for device, at in enumerate(COORDS)}
    return [(device, index[move(*at)]) for device, at in enumerate(COORDS)]


BRICK = groups(
    lambda x, y, z, c: (y // 2, z // 2, c), lambda x, y, z, c: (x, y % 2, z % 2)
)
STRANDS = ((0, 2, 5, 7), (1, 3, 4, 6))
STRAND = tuple(int(place in STRANDS[1]) for place in range(8))
FAR_Y = lambda x, y, z, c: (c, x, STRAND[y], z)
FAR_Z = lambda x, y, z, c: (c, x, y, STRAND[z])
FAR_FIRST = groups(
    lambda *at: FAR_Z(*at) if at[3] else FAR_Y(*at), lambda x, y, z, c: z if c else y
)
FAR_SECOND = groups(
    lambda *at: FAR_Y(*at) if at[3] else FAR_Z(*at), lambda x, y, z, c: y if c else z
)


def place(device, k, q):
    x, y, z = device & 3, (device >> 5) & 1, (device >> 2) & 1
    return 4 * ((x - SHIFTS[k]) & 3) + ((2 * y + z) ^ q)


def split(a):
    hi = a.astype(jnp.bfloat16)
    return hi, (a - hi.astype(jnp.float32)).astype(jnp.bfloat16)


def dot(a, b, dims):
    return lax.dot_general(a, b, dims, preferred_element_type=jnp.float32)


def add_columns(col_ref, inv, row_x3, row_w3, row_q, pulls, sums, fresh):
    width = inv.shape[1]
    for start in range(0, col_ref.shape[0], CHUNK):
        col = col_ref[start : start + CHUNK, :]
        col_x = col[:, :width]
        x_hi, x_lo = split(col_x)
        w_hi, w_lo = split(col[:, width:])
        half = -0.5 * jnp.sum(col_x * col_x * inv, axis=1, keepdims=True)
        col_q = jnp.transpose(jnp.broadcast_to(half, (CHUNK, LANES)))[:1]
        inner = dot(row_x3[...], jnp.concatenate([x_hi, x_hi, x_lo], axis=1), NT)
        mixing = dot(row_w3[...], jnp.concatenate([w_hi, w_hi, w_lo], axis=1), NT)
        parts = CHUNK // LANES
        q = jnp.concatenate([row_q] * parts, axis=1) + col_q
        coupling = mixing * jnp.exp(inner + q)
        c_hi, c_lo = split(coupling)
        for part in range(parts):
            piece = coupling[:, part * LANES : (part + 1) * LANES]
            sums = piece if sums is None else sums + piece
        pulled = dot(
            jnp.concatenate([c_hi, c_lo, c_hi], axis=1),
            jnp.concatenate([x_hi, x_hi, x_lo], axis=0),
            NN,
        )
        if fresh and start == 0:
            pulls[...] = pulled
        else:
            pulls[...] += pulled
    return sums


def near_kernel(inv_ref, r0, r1, r2, r3, col_ref, pulls, sum_ref, q_ref, row_x3, row_w3):
    width = inv_ref.shape[1]
    rank = (col_ref.shape[1] - width) // 2
    inv = inv_ref[...]
    for k, row_ref in enumerate((r0, r1, r2, r3)):
        count = row_ref.shape[0]
        at = slice(k * count, (k + 1) * count)
        x = row_ref[:, :width]
        scaled = x * inv
        half = -0.5 * jnp.sum(scaled * x, axis=1, keepdims=True)
        q_ref[at, :] = jnp.broadcast_to(half, (count, LANES))
        hi, lo = split(scaled)
        row_x3[at, :] = jnp.concatenate([hi, lo, hi], axis=1)
        hi, lo = split(pltpu.roll(row_ref[:, width:], rank, 1))
        row_w3[at, :] = jnp.concatenate([hi, lo, hi], axis=1)
    sum_ref[...] = add_columns(col_ref, inv, row_x3, row_w3, q_ref[...], pulls, None, True)


def other_kernel(
    inv_ref, r0, r1, r2, r3, col_ref, near_pulls, near_sums, q_ref, row_x3, row_w3, out_ref, pulls
):
    width = inv_ref.shape[1]
    inv = inv_ref[...]
    sums = add_columns(col_ref, inv, row_x3, row_w3, q_ref[...], pulls, near_sums[...], True)
    total = jnp.sum(sums, axis=1, keepdims=True)
    device = lax.axis_index(AXIS)
    for k, row_ref in enumerate((r0, r1, r2, r3)):
        count = row_ref.shape[0] // 4
        for q in range(4):
            at = slice((4 * k + q) * count, (4 * k + q + 1) * count)
            where = pl.ds(pl.multiple_of(place(device, k, q) * count, count), count)
            x = row_ref[q * count : (q + 1) * count, :width]
            pulled = near_pulls[at, :] + pulls[at, :]
            out_ref[where, :] = (pulled - total[at, :] * x) * inv


def on_chip(kernel, out_shape, scratch_shapes, *args):
    vmem = pl.BlockSpec(memory_space=pltpu.VMEM)
    return pl.pallas_call(
        kernel,
        in_specs=[vmem] * len(args),
        out_specs=[vmem] * len(out_shape),
        out_shape=out_shape,
        scratch_shapes=scratch_shapes,
        compiler_params=pltpu.CompilerParams(vmem_limit_bytes=24 * 2**20),
    )(args[0], *(pltpu.with_memory_space_constraint(arg, pltpu.VMEM) for arg in args[1:]))


def exchange(blocks, members):
    return lax.all_to_all(blocks, AXIS, 0, 0, axis_index_groups=members, tiled=True)


def spread(block, members):
    copies = jnp.broadcast_to(block[None], (len(members[0]), *block.shape))
    return exchange(copies, members).reshape(-1, block.shape[-1])


def send(block, move):
    return lax.ppermute(block, AXIS, pairs(move))


def on_device(features, inv_scale, probe_u, solve_v):
    local, width = features.shape
    own = jnp.concatenate([features, probe_u, solve_v], axis=1)
    far, *partners = lax.optimization_barrier(
        (
            spread(own, FAR_FIRST),
            send(own, lambda x, y, z, c: (x, y, z ^ 1, c)),
            send(own, lambda x, y, z, c: (x, y ^ 1, z, c)),
            send(own, lambda x, y, z, c: (x, y ^ 1, z ^ 1, c)),
        )
    )
    quad = jnp.concatenate([own, *partners])
    near, *ring = lax.optimization_barrier(
        (
            spread(far, FAR_SECOND),
            *(
                send(quad, lambda x, y, z, c, by=by: ((x + by) % 4, y, z, c))
                for by in SHIFTS[1:]
            ),
        )
    )
    other = send(near, lambda x, y, z, c: (x, y, z, 1 - c))
    inv = inv_scale.reshape(1, width)
    rows = [quad, *ring]
    count = len(BRICK[0]) * local
    pulls = pltpu.VMEM((count, width), jnp.float32)
    lanes = pltpu.VMEM((count, LANES), jnp.float32)
    row_x3 = pltpu.VMEM((count, 3 * width), jnp.bfloat16)
    row_w3 = pltpu.VMEM((count, 3 * (own.shape[1] - width)), jnp.bfloat16)
    half = on_chip(near_kernel, [pulls, lanes, lanes, row_x3, row_w3], [], inv, *rows, near)
    (terms,) = on_chip(other_kernel, [pulls], [pulls], inv, *rows, other, *half)
    shares = exchange(terms.reshape(len(BRICK[0]), local, width), BRICK)
    return jnp.sum(shares, axis=0)


def solution(mesh):
    return jax.shard_map(
        on_device,
        mesh=Mesh(mesh.devices.reshape(-1), (AXIS,)),
        in_specs=(P(AXIS, None), P(), P(AXIS, None), P(AXIS, None)),
        out_specs=P(AXIS, None),
        check_vma=False,
    )
```

```python
import jax
import jax.numpy as jnp
from jax import lax
from jax.experimental import pallas as pl
from jax.experimental.pallas import tpu as pltpu
from jax.sharding import Mesh, PartitionSpec as P


NT = (((1,), (1,)), ((), ()))
NN = (((1,), (0,)), ((), ()))
LANES = 128
CHUNK = 256

AXIS = "device"
SHIFTS = (0, 1, -1, 2)
COORDS = tuple(
    (x, y, 4 * z_hi + z_lo, core)
    for z_hi in range(2)
    for y in range(8)
    for core in range(2)
    for z_lo in range(4)
    for x in range(4)
)


def groups(key, place):
    found = {}
    for device, at in enumerate(COORDS):
        found.setdefault(key(*at), []).append((place(*at), device))
    return [[device for _, device in sorted(found[k])] for k in sorted(found)]


def pairs(move):
    index = {at: device for device, at in enumerate(COORDS)}
    return [(device, index[move(*at)]) for device, at in enumerate(COORDS)]


BRICK = groups(
    lambda x, y, z, c: (y // 2, z // 2, c), lambda x, y, z, c: (x, y % 2, z % 2)
)
STRANDS = ((0, 2, 5, 7), (1, 3, 4, 6))
STRAND = tuple(int(place in STRANDS[1]) for place in range(8))
FAR_Y = lambda x, y, z, c: (c, x, STRAND[y], z)
FAR_Z = lambda x, y, z, c: (c, x, y, STRAND[z])
FAR_FIRST = groups(
    lambda *at: FAR_Z(*at) if at[3] else FAR_Y(*at), lambda x, y, z, c: z if c else y
)
FAR_SECOND = groups(
    lambda *at: FAR_Y(*at) if at[3] else FAR_Z(*at), lambda x, y, z, c: y if c else z
)


def place(device, k, q):
    x, y, z = device & 3, (device >> 5) & 1, (device >> 2) & 1
    return 4 * ((x - SHIFTS[k]) & 3) + ((2 * y + z) ^ q)


def split(a):
    hi = a.astype(jnp.bfloat16)
    return hi, (a - hi.astype(jnp.float32)).astype(jnp.bfloat16)


def dot(a, b, dims):
    return lax.dot_general(a, b, dims, preferred_element_type=jnp.float32)


def add_columns(col_ref, inv, row_x3, row_w3, row_q, pulls, sums, fresh):
    width = inv.shape[1]
    for start in range(0, col_ref.shape[0], CHUNK):
        col = col_ref[start : start + CHUNK, :]
        col_x = col[:, :width]
        x_hi, x_lo = split(col_x)
        w_hi, w_lo = split(col[:, width:])
        half = -0.5 * jnp.sum(col_x * col_x * inv, axis=1, keepdims=True)
        col_q = jnp.transpose(jnp.broadcast_to(half, (CHUNK, LANES)))[:1]
        inner = dot(row_x3[...], jnp.concatenate([x_hi, x_hi, x_lo], axis=1), NT)
        mixing = dot(row_w3[...], jnp.concatenate([w_hi, w_hi, w_lo], axis=1), NT)
        parts = CHUNK // LANES
        q = jnp.concatenate([row_q] * parts, axis=1) + col_q
        coupling = mixing * jnp.exp(inner + q)
        c_hi, c_lo = split(coupling)
        for part in range(parts):
            piece = coupling[:, part * LANES : (part + 1) * LANES]
            sums = piece if sums is None else sums + piece
        pulled = dot(
            jnp.concatenate([c_hi, c_lo, c_hi], axis=1),
            jnp.concatenate([x_hi, x_hi, x_lo], axis=0),
            NN,
        )
        if fresh and start == 0:
            pulls[...] = pulled
        else:
            pulls[...] += pulled
    return sums


def near_kernel(inv_ref, r0, r1, r2, r3, col_ref, pulls, sum_ref, q_ref, row_x3, row_w3):
    width = inv_ref.shape[1]
    rank = (col_ref.shape[1] - width) // 2
    inv = inv_ref[...]
    for k, row_ref in enumerate((r0, r1, r2, r3)):
        count = row_ref.shape[0]
        at = slice(k * count, (k + 1) * count)
        x = row_ref[:, :width]
        scaled = x * inv
        half = -0.5 * jnp.sum(scaled * x, axis=1, keepdims=True)
        q_ref[at, :] = jnp.broadcast_to(half, (count, LANES))
        hi, lo = split(scaled)
        row_x3[at, :] = jnp.concatenate([hi, lo, hi], axis=1)
        hi, lo = split(pltpu.roll(row_ref[:, width:], rank, 1))
        row_w3[at, :] = jnp.concatenate([hi, lo, hi], axis=1)
    sum_ref[...] = add_columns(col_ref, inv, row_x3, row_w3, q_ref[...], pulls, None, True)


def other_kernel(
    inv_ref, r0, r1, r2, r3, col_ref, near_pulls, near_sums, q_ref, row_x3, row_w3, out_ref, pulls
):
    width = inv_ref.shape[1]
    inv = inv_ref[...]
    sums = add_columns(col_ref, inv, row_x3, row_w3, q_ref[...], pulls, near_sums[...], True)
    total = jnp.sum(sums, axis=1, keepdims=True)
    device = lax.axis_index(AXIS)
    for k, row_ref in enumerate((r0, r1, r2, r3)):
        count = row_ref.shape[0] // 4
        for q in range(4):
            at = slice((4 * k + q) * count, (4 * k + q + 1) * count)
            where = pl.ds(pl.multiple_of(place(device, k, q) * count, count), count)
            x = row_ref[q * count : (q + 1) * count, :width]
            pulled = near_pulls[at, :] + pulls[at, :]
            out_ref[where, :] = (pulled - total[at, :] * x) * inv


def on_chip(kernel, out_shape, scratch_shapes, *args):
    vmem = pl.BlockSpec(memory_space=pltpu.VMEM)
    return pl.pallas_call(
        kernel,
        in_specs=[vmem] * len(args),
        out_specs=[vmem] * len(out_shape),
        out_shape=out_shape,
        scratch_shapes=scratch_shapes,
        compiler_params=pltpu.CompilerParams(vmem_limit_bytes=24 * 2**20),
    )(args[0], *(pltpu.with_memory_space_constraint(arg, pltpu.VMEM) for arg in args[1:]))


def pack_kernel(x_ref, u_ref, v_ref, own_ref, copies_ref):
    width, rank = x_ref.shape[1], u_ref.shape[1]
    own_ref[:, :width] = x_ref[...]
    own_ref[:, width : width + rank] = u_ref[...]
    own_ref[:, width + rank :] = v_ref[...]
    own = own_ref[...]
    for k in range(copies_ref.shape[0]):
        copies_ref[k] = own


def copy_kernel(block_ref, copies_ref):
    block = block_ref[...]
    for k in range(copies_ref.shape[0]):
        copies_ref[k] = block


def small_call(kernel, out_shape, *args):
    vmem = pl.BlockSpec(memory_space=pltpu.VMEM)
    return pl.pallas_call(
        kernel,
        in_specs=[vmem] * len(args),
        out_specs=[vmem] * len(out_shape),
        out_shape=[pltpu.VMEM(shape, jnp.float32) for shape in out_shape],
        compiler_params=pltpu.CompilerParams(vmem_limit_bytes=8 * 2**20),
    )(*args)


def exchange(blocks, members):
    return lax.all_to_all(blocks, AXIS, 0, 0, axis_index_groups=members, tiled=True)


def send(block, move):
    return lax.ppermute(block, AXIS, pairs(move))


def on_device(features, inv_scale, probe_u, solve_v):
    local, width = features.shape
    packed = width + probe_u.shape[1] + solve_v.shape[1]
    own, copies = small_call(
        pack_kernel, [(local, packed), (4, local, packed)], features, probe_u, solve_v
    )
    far = exchange(copies, FAR_FIRST).reshape(4 * local, packed)
    quad = [own]
    for k in (1, 2, 3):
        quad.append(send(own, lambda x, y, z, c, k=k: (x, y ^ k // 2, z ^ k % 2, c)))
    quad = jnp.concatenate(quad)
    far = pltpu.with_memory_space_constraint(far, pltpu.VMEM)
    (copies,) = small_call(copy_kernel, [(4, 4 * local, packed)], far)
    near = exchange(copies, FAR_SECOND).reshape(16 * local, packed)
    ring = []
    for by in SHIFTS[1:]:
        ring.append(send(quad, lambda x, y, z, c, by=by: ((x + by) % 4, y, z, c)))
    other = send(near, lambda x, y, z, c: (x, y, z, 1 - c))
    inv = inv_scale.reshape(1, width)
    rows = [quad, *ring]
    count = len(BRICK[0]) * local
    pulls = pltpu.VMEM((count, width), jnp.float32)
    lanes = pltpu.VMEM((count, LANES), jnp.float32)
    row_x3 = pltpu.VMEM((count, 3 * width), jnp.bfloat16)
    row_w3 = pltpu.VMEM((count, 3 * (own.shape[1] - width)), jnp.bfloat16)
    half = on_chip(near_kernel, [pulls, lanes, lanes, row_x3, row_w3], [], inv, *rows, near)
    (terms,) = on_chip(other_kernel, [pulls], [pulls], inv, *rows, other, *half)
    shares = exchange(terms.reshape(len(BRICK[0]), local, width), BRICK)
    return jnp.sum(shares, axis=0)


def solution(mesh):
    return jax.shard_map(
        on_device,
        mesh=Mesh(mesh.devices.reshape(-1), (AXIS,)),
        in_specs=(P(AXIS, None), P(), P(AXIS, None), P(AXIS, None)),
        out_specs=P(AXIS, None),
        check_vma=False,
    )
```

```python
import jax
import jax.numpy as jnp
from jax import lax
from jax.experimental import pallas as pl
from jax.experimental.pallas import tpu as pltpu
from jax.sharding import Mesh, PartitionSpec as P


NT = (((1,), (1,)), ((), ()))
NN = (((1,), (0,)), ((), ()))
LANES = 128
CHUNK = 256

AXIS = "device"
SHIFTS = (0, 1, -1, 2)
COORDS = tuple(
    (x, y, 4 * z_hi + z_lo, core)
    for z_hi in range(2)
    for y in range(8)
    for core in range(2)
    for z_lo in range(4)
    for x in range(4)
)


def groups(key, place):
    found = {}
    for device, at in enumerate(COORDS):
        found.setdefault(key(*at), []).append((place(*at), device))
    return [[device for _, device in sorted(found[k])] for k in sorted(found)]


def pairs(move):
    index = {at: device for device, at in enumerate(COORDS)}
    return [(device, index[move(*at)]) for device, at in enumerate(COORDS)]


BRICK = groups(
    lambda x, y, z, c: (y // 2, z // 2, c), lambda x, y, z, c: (z % 2, x, y % 2)
)
STRANDS = ((0, 2, 5, 7), (1, 3, 4, 6))
STRAND = tuple(int(place in STRANDS[1]) for place in range(8))
FAR_Y = lambda x, y, z, c: (c, x, STRAND[y], z)
FAR_Z = lambda x, y, z, c: (c, x, y, STRAND[z])
FAR_FIRST = groups(
    lambda *at: FAR_Z(*at) if at[3] else FAR_Y(*at), lambda x, y, z, c: z if c else y
)
FAR_SECOND = groups(
    lambda *at: FAR_Y(*at) if at[3] else FAR_Z(*at), lambda x, y, z, c: y if c else z
)


def place(device, k, q):
    x, y, z = device & 3, (device >> 5) & 1, (device >> 2) & 1
    return 8 * (z ^ (q & 1)) + 2 * ((x - SHIFTS[k]) & 3) + (y ^ (q >> 1))


def split(a):
    hi = a.astype(jnp.bfloat16)
    return hi, (a - hi.astype(jnp.float32)).astype(jnp.bfloat16)


def dot(a, b, dims):
    return lax.dot_general(a, b, dims, preferred_element_type=jnp.float32)


def add_columns(col_ref, inv, row_x3, row_w3, row_q, pulls, sums, fresh):
    width = inv.shape[1]
    for start in range(0, col_ref.shape[0], CHUNK):
        col = col_ref[start : start + CHUNK, :]
        col_x = col[:, :width]
        x_hi, x_lo = split(col_x)
        w_hi, w_lo = split(col[:, width:])
        half = -0.5 * jnp.sum(col_x * col_x * inv, axis=1, keepdims=True)
        col_q = jnp.transpose(jnp.broadcast_to(half, (CHUNK, LANES)))[:1]
        inner = dot(row_x3[...], jnp.concatenate([x_hi, x_hi, x_lo], axis=1), NT)
        mixing = dot(row_w3[...], jnp.concatenate([w_hi, w_hi, w_lo], axis=1), NT)
        parts = CHUNK // LANES
        q = jnp.concatenate([row_q] * parts, axis=1) + col_q
        coupling = mixing * jnp.exp(inner + q)
        c_hi, c_lo = split(coupling)
        for part in range(parts):
            piece = coupling[:, part * LANES : (part + 1) * LANES]
            sums = piece if sums is None else sums + piece
        pulled = dot(
            jnp.concatenate([c_hi, c_lo, c_hi], axis=1),
            jnp.concatenate([x_hi, x_hi, x_lo], axis=0),
            NN,
        )
        if fresh and start == 0:
            pulls[...] = pulled
        else:
            pulls[...] += pulled
    return sums


def near_kernel(inv_ref, r0, r1, r2, r3, col_ref, pulls, sum_ref, q_ref, row_x3, row_w3):
    width = inv_ref.shape[1]
    rank = (col_ref.shape[1] - width) // 2
    inv = inv_ref[...]
    for k, row_ref in enumerate((r0, r1, r2, r3)):
        count = row_ref.shape[0]
        at = slice(k * count, (k + 1) * count)
        x = row_ref[:, :width]
        scaled = x * inv
        half = -0.5 * jnp.sum(scaled * x, axis=1, keepdims=True)
        q_ref[at, :] = jnp.broadcast_to(half, (count, LANES))
        hi, lo = split(scaled)
        row_x3[at, :] = jnp.concatenate([hi, lo, hi], axis=1)
        hi, lo = split(pltpu.roll(row_ref[:, width:], rank, 1))
        row_w3[at, :] = jnp.concatenate([hi, lo, hi], axis=1)
    sum_ref[...] = add_columns(col_ref, inv, row_x3, row_w3, q_ref[...], pulls, None, True)


def other_kernel(
    inv_ref, r0, r1, r2, r3, col_ref, near_pulls, near_sums, q_ref, row_x3, row_w3, out_ref, pulls
):
    width = inv_ref.shape[1]
    inv = inv_ref[...]
    sums = add_columns(col_ref, inv, row_x3, row_w3, q_ref[...], pulls, near_sums[...], True)
    total = jnp.sum(sums, axis=1, keepdims=True)
    device = lax.axis_index(AXIS)
    for k, row_ref in enumerate((r0, r1, r2, r3)):
        count = row_ref.shape[0] // 4
        for q in range(4):
            at = slice((4 * k + q) * count, (4 * k + q + 1) * count)
            where = pl.ds(pl.multiple_of(place(device, k, q) * count, count), count)
            x = row_ref[q * count : (q + 1) * count, :width]
            pulled = near_pulls[at, :] + pulls[at, :]
            out_ref[where, :] = (pulled - total[at, :] * x) * inv


def on_chip(kernel, out_shape, scratch_shapes, *args):
    vmem = pl.BlockSpec(memory_space=pltpu.VMEM)
    return pl.pallas_call(
        kernel,
        in_specs=[vmem] * len(args),
        out_specs=[vmem] * len(out_shape),
        out_shape=out_shape,
        scratch_shapes=scratch_shapes,
        compiler_params=pltpu.CompilerParams(vmem_limit_bytes=24 * 2**20),
    )(args[0], *(pltpu.with_memory_space_constraint(arg, pltpu.VMEM) for arg in args[1:]))


def exchange(blocks, members):
    return lax.all_to_all(blocks, AXIS, 0, 0, axis_index_groups=members, tiled=True)


def spread(block, members):
    copies = jnp.broadcast_to(block[None], (len(members[0]), *block.shape))
    return exchange(copies, members).reshape(-1, block.shape[-1])


def send(block, move):
    return lax.ppermute(block, AXIS, pairs(move))


def on_device(features, inv_scale, probe_u, solve_v):
    local, width = features.shape
    own = jnp.concatenate([features, probe_u, solve_v], axis=1)
    far = spread(own, FAR_FIRST)
    quad = [own]
    for k in (1, 2, 3):
        quad.append(send(own, lambda x, y, z, c, k=k: (x, y ^ k // 2, z ^ k % 2, c)))
    quad = jnp.concatenate(quad)
    near = spread(far, FAR_SECOND)
    ring = []
    for by in SHIFTS[1:]:
        ring.append(send(quad, lambda x, y, z, c, by=by: ((x + by) % 4, y, z, c)))
    other = send(near, lambda x, y, z, c: (x, y, z, 1 - c))
    inv = inv_scale.reshape(1, width)
    rows = [quad, *ring]
    count = len(BRICK[0]) * local
    pulls = pltpu.VMEM((count, width), jnp.float32)
    lanes = pltpu.VMEM((count, LANES), jnp.float32)
    row_x3 = pltpu.VMEM((count, 3 * width), jnp.bfloat16)
    row_w3 = pltpu.VMEM((count, 3 * (own.shape[1] - width)), jnp.bfloat16)
    half = on_chip(near_kernel, [pulls, lanes, lanes, row_x3, row_w3], [], inv, *rows, near)
    (terms,) = on_chip(other_kernel, [pulls], [pulls], inv, *rows, other, *half)
    shares = exchange(terms.reshape(len(BRICK[0]), local, width), BRICK)
    return jnp.sum(shares, axis=0)


def solution(mesh):
    return jax.shard_map(
        on_device,
        mesh=Mesh(mesh.devices.reshape(-1), (AXIS,)),
        in_specs=(P(AXIS, None), P(), P(AXIS, None), P(AXIS, None)),
        out_specs=P(AXIS, None),
        check_vma=False,
    )
```
